32 devices in a mesh: col: 8 (over y, x, core), row: 4 (over z).
Axes of the slice: x: 2, y: 2, z: 4, core: 2. Of those that a mesh axis runs over, the one named last changes fastest.
Arguments:
- w_tiles: bfloat16 [32, 512, 512], P(('col', 'row')), may hold values from -0.09375 to 0.09375
- task_ab: int32 [32], P(('col', 'row')), may hold values from 0 to 3, as said below
- task_ef: int32 [32], P(('col', 'row')), may hold values from 0 to 7
- lam_pairs: bfloat16 [16384, 4096], P('row', 'col'), may hold values from -6 to 6
- other_terms: bfloat16 [2048, 4096], P('row', 'col'), may hold values from -6 to 6
- vir_pair: float32 [2048], P('row'), may hold values from 1 to 4
- occ_pair: float32 [4096], P('col'), may hold values from -3 to -1
Outputs:
- lam_new: bfloat16 [2048, 4096], P('row', 'col')
The draws below stay inside these ranges and needn't reach their ends.
Inputs may be any that keep to these rules, and one draw needn't show every extreme that they name: Within one row group no pair (task_ab, task_ef) is listed twice.
All inputs are finite; a program needn't handle non-finite values.
Results may differ from the reference program's by a relative error of at most 0.001.
Values may be sent and summed in bfloat16 or wider, within the bound.
No kernel may reach another device: no remote copies, remote signals or barrier semaphores. Data moves between devices by JAX's collectives and lax.ppermute only.
A program may use at most 64 MiB of HBM per device.

```python
import jax
import jax.numpy as jnp
from jax import lax

TILE = 512
AB_T = 4
EF_DEV_T = 8
TASK_DEV = 1
AB = 2048
EF = 16384
IJ = 4096
TASKS = 32
N_COL = 8
N_ROW = 4


def block_ids(key):
    block_total = AB_T * EF_DEV_T
    group_keys = jax.random.split(jax.random.fold_in(key, 7151), N_ROW)
    perms = jax.vmap(lambda k: jax.random.permutation(k, block_total))(group_keys).astype(jnp.int32)
    order = jnp.arange(TASKS, dtype=jnp.int32)
    device = order // TASK_DEV
    group = device % N_ROW
    within = device // N_ROW * TASK_DEV + order % TASK_DEV
    return perms[group, within].astype(jnp.int32)


def draw_task_ab(key, part):
    return (block_ids(key) // EF_DEV_T).astype(jnp.int32)


def draw_task_ef(key, part):
    return (block_ids(key) % EF_DEV_T).astype(jnp.int32)


def shard_levels(key, dims, cuts, low, largest):
    loudness, own = 1.0, jax.random.fold_in(key, 6)
    for position, blocks in cuts:
        steps = jnp.exp(jax.random.uniform(jax.random.fold_in(own, position), (blocks,), jnp.float32, low / len(cuts), largest / len(cuts)))
        loudness = loudness * jnp.repeat(steps, dims[position] // blocks).reshape([-1 if axis == position else 1 for axis in range(len(dims))])
    return loudness


def gaussian(rng, extent, scale, most, shards=(), kind=jnp.bfloat16):
    array = jax.random.normal(rng, extent, jnp.float32) * scale
    if len(shards) > 0:
        array = shard_levels(rng, extent, shards, -0.22, 0.18) * array
    return jnp.clip(array, min=-most, max=most).astype(kind)


def setup_inputs(seed: int = 0) -> dict:
    seeds = jax.random.split(jax.random.key(seed), 8)
    w_tiles = gaussian(seeds[0], (TASKS, TILE, TILE), (TILE * TASK_DEV * N_COL * N_ROW // AB_T) ** -0.5, 0.09375, ((0, 32),))
    task_ab = draw_task_ab(jax.random.fold_in(seeds[7], 71), 0)
    task_ef = draw_task_ef(jax.random.fold_in(seeds[7], 71), 0)
    lam_pairs = gaussian(seeds[3], (EF, IJ), 1.0, 6.0, ((0, 4), (1, 8)))
    other_terms = gaussian(seeds[4], (AB, IJ), 1.0, 6.0, ((0, 4), (1, 8)))
    vir_pair = jnp.clip(1.0 + 3.0 * jax.random.uniform(seeds[5], (AB,), jnp.float32) ** shard_levels(seeds[5], (AB,), ((0, 4),), -0.2, 0.2), 1.0, 4.0)
    occ_pair = jnp.clip(-3.0 + 2.0 * jax.random.uniform(seeds[6], (IJ,), jnp.float32) ** shard_levels(seeds[6], (IJ,), ((0, 8),), -0.2, 0.2), -3.0, -1.0)
    return {"w_tiles": w_tiles, "task_ab": task_ab, "task_ef": task_ef, "lam_pairs": lam_pairs, "other_terms": other_terms, "vir_pair": vir_pair, "occ_pair": occ_pair}


def reference(w_tiles, task_ab, task_ef, lam_pairs, other_terms, vir_pair, occ_pair):
    col_count = lam_pairs.shape[1]
    lam_blocks = lam_pairs.astype(jnp.float32).reshape(N_ROW * EF_DEV_T, TILE, col_count)
    order = jnp.arange(TASKS, dtype=jnp.int32)
    group = (order // TASK_DEV) % N_ROW
    ef_tile = (group * EF_DEV_T + task_ef).astype(jnp.int32)

    def step(totals, items):
        tile_now, ab_id, ef_id = items
        block = lax.dynamic_index_in_dim(lam_blocks, ef_id, 0, keepdims=False)
        product = jnp.dot(tile_now.astype(jnp.float32), block, precision=lax.Precision.HIGHEST)
        totals = totals.at[ab_id].add(product)
        return totals, None

    start = jnp.zeros((AB_T, TILE, col_count), jnp.float32)
    totals, unused = lax.scan(step, start, (w_tiles, task_ab.astype(jnp.int32), ef_tile))
    ladder = totals.reshape(AB_T * TILE, col_count)
    combined = other_terms.astype(jnp.float32) + ladder
    denominator = occ_pair[None, :] - vir_pair[:, None]
    return (combined / denominator).astype(jnp.bfloat16)
```

```python
import functools

import jax
import jax.numpy as jnp
from jax import lax
from jax.experimental import pallas as pl
from jax.experimental.pallas import tpu as pltpu
from jax.sharding import PartitionSpec as P

SPLIT = (0.25, 0.625)
HEAD = 8


def chunk_bounds(rows):
    cuts = [0] + [max(16, int(rows * s) // 16 * 16) for s in SPLIT] + [rows]
    return [(a, b) for a, b in zip(cuts[:-1], cuts[1:]) if b > a]


def ladder_kernel(count, row_count, offset, *refs):
    pieces, heads = refs[:count], refs[count : 2 * count]
    lam = refs[2 * count]
    outs = refs[2 * count + 1 : 2 * count + 1 + row_count]
    buf, totals, sems = refs[2 * count + 1 + row_count :]
    depth = buf.shape[1]
    ef_count = lam.shape[0] // depth
    height = pieces[0].shape[0] - offset
    codes, copies = [], []
    for t in range(count):
        code = jnp.max(heads[t][...].astype(jnp.float32)).astype(jnp.int32)
        ef = code % ef_count
        codes.append(code // ef_count)
        copy = pltpu.make_async_copy(
            lam.at[pl.ds(pl.multiple_of(ef * depth, depth), depth), :], buf.at[t], sems.at[t]
        )
        copy.start()
        copies.append(copy)
    totals[...] = jnp.zeros_like(totals)
    for t in range(count):
        copies[t].wait()
        product = jnp.dot(
            pieces[t][pl.ds(offset, height), :], buf[t], preferred_element_type=jnp.float32
        )
        rows = pl.ds(pl.multiple_of(codes[t] * height, height), height)
        totals[rows, :] += product
    me = lax.axis_index("row")
    own = totals.shape[0] // row_count
    for j in range(row_count):
        other = lax.bitwise_xor(me, j)
        outs[j][...] = totals[pl.ds(pl.multiple_of(other * own, own), own), :]


def ladder_chunk(pieces, heads, lam, row_count, ab_tiles, depth, offset):
    count = len(pieces)
    height = pieces[0].shape[0] - offset
    width = lam.shape[1]
    own = ab_tiles * height // row_count
    vmem = pl.BlockSpec(memory_space=pltpu.VMEM)
    head_spec = pl.BlockSpec((HEAD, heads[0].shape[1]), lambda i: (0, 0))
    flops = 2 * count * height * depth * width
    return pl.pallas_call(
        functools.partial(ladder_kernel, count, row_count, offset),
        grid=(1,),
        out_shape=[jax.ShapeDtypeStruct((own, width), jnp.float32)] * row_count,
        in_specs=[vmem] * count + [head_spec] * count + [pl.BlockSpec(memory_space=pl.ANY)],
        out_specs=[vmem] * row_count,
        scratch_shapes=[
            pltpu.VMEM((count, depth, width), lam.dtype),
            pltpu.VMEM((ab_tiles * height, width), jnp.float32),
            pltpu.SemaphoreType.DMA((count,)),
        ],
        compiler_params=pltpu.CompilerParams(vmem_limit_bytes=36 * 2**20),
        cost_estimate=pl.CostEstimate(
            flops=flops, bytes_accessed=count * depth * width * 2, transcendentals=0
        ),
    )(*pieces, *heads, lam)


def body(row_count, col_count, w_tiles, task_ab, task_ef, lam, other, vir, occ):
    tasks, tile_rows, depth = w_tiles.shape
    own_rows = other.shape[0]
    ab_tiles = own_rows * row_count // tile_rows
    sub = tile_rows // own_rows
    ef_count = lam.shape[0] // depth

    def send(x, axis, count, k):
        return lax.ppermute(x, axis, [(i, i ^ k) for i in range(count)])

    bounds = chunk_bounds(own_rows)
    code = (task_ab * ef_count + task_ef).astype(jnp.bfloat16)
    w_rows = w_tiles.reshape(tasks, sub, own_rows, depth)
    bases = []
    for index, (a, b) in enumerate(bounds):
        for t in range(tasks):
            part = w_rows[t, :, a:b].reshape(sub * (b - a), depth)
            if index == 0:
                part = jnp.concatenate([jnp.broadcast_to(code[t], (HEAD, depth)), part], 0)
            bases.append((index, part))
    gathered = {}
    for index, part in bases:
        near = [part] + [send(part, "col", col_count, k) for k in range(2, col_count, 2)]
        gathered.setdefault(index, []).extend(near)
    partial = []
    heads = None
    for index, (a, b) in enumerate(bounds):
        near = gathered[index]
        pieces = near + [send(x, "col", col_count, 1) for x in near]
        heads = pieces if index == 0 else heads
        partial.append(
            ladder_chunk(
                pieces, heads, lam, row_count, ab_tiles, depth, HEAD if index == 0 else 0
            )
        )
    results = []
    for index, (a, b) in enumerate(bounds):
        blocks = partial[index]
        step = 1
        while step < row_count:
            away = jnp.stack([x.astype(jnp.float16) for x in blocks[1::2]])
            here = send(away, "row", row_count, step)
            blocks = [x + here[i].astype(jnp.float32) for i, x in enumerate(blocks[0::2])]
            step *= 2
        combined = other[a:b].astype(jnp.float32) + blocks[0]
        denominator = occ[None, :] - vir[a:b, None]
        results.append((combined / denominator).astype(jnp.bfloat16))
    return jnp.concatenate(results, 0)


def solution(mesh):
    placed = (
        P(("col", "row"), None, None),
        P(("col", "row")),
        P(("col", "row")),
        P("row", "col"),
        P("row", "col"),
        P("row"),
        P("col"),
    )
    return jax.shard_map(
        functools.partial(body, mesh.shape["row"], mesh.shape["col"]),
        mesh=mesh,
        in_specs=placed,
        out_specs=P("row", "col"),
        check_vma=False,
    )
```
